32 devices in a mesh: layer: 4 (over x, core), latent: 8 (over z, y).
Axes of the slice: x: 2, y: 2, z: 4, core: 2. Of those that a mesh axis runs over, the one named last changes fastest.
Arguments:
- acts: bfloat16 [4, 512, 2048], P('layer', None, 'latent'), may hold values from -6 to 6
- w_enc: bfloat16 [4, 2048, 4096], P('layer', None, 'latent'), may hold values from -0.0625 to 0.0625
- b_enc: float32 [4096], P('latent'), may hold values from -3 to 3
- w_dec: bfloat16 [4, 4096, 2048], P('layer', 'latent'), may hold values from -0.125 to 0.125
- b_dec: bfloat16 [4, 2048], P('layer', 'latent'), may hold values from -3 to 3
Outputs:
- grad_enc: bfloat16 [4, 2048, 4096], P('layer', None, 'latent')
- grad_dec: bfloat16 [4, 4096, 2048], P('layer', 'latent')
- grad_benc: float32 [4096], P('latent')
- grad_bdec: float32 [4, 2048], P('layer', 'latent')
The draws below stay inside these ranges and needn't reach their ends.
All inputs are finite; a program needn't handle non-finite values.
Results may differ from the reference program's by a relative error of at most 0.014.
Values may be sent and summed in bfloat16 or wider, within the bound.
A program may use at most 64 MiB of HBM per device.

```python
import jax
import jax.numpy as jnp

D = 4096
LAYERS = 2
TOK = 512
LATENTS = 4096


def with_spikes(entries, rng, source, target, shards_of, factor):
    def block_of(position):
        return (jnp.arange(entries.shape[position]) // (entries.shape[position] // shards_of)).reshape((-1,) + (1,) * (entries.ndim - 1 - position))

    near = jax.random.permutation(rng, shards_of)[block_of(target)]
    second = (block_of(target) + shards_of // 2) % shards_of
    return jnp.where((block_of(source) == near) | (block_of(source) == second), factor * entries, entries)


def levels(key, dims, shards, low, top_value):
    factor_of, own = 1.0, jax.random.fold_in(key, 6)
    for axis_at, blocks in shards:
        heights = jnp.exp(jax.random.uniform(jax.random.fold_in(own, axis_at), (blocks,), jnp.float32, low / len(shards), top_value / len(shards)))
        factor_of = factor_of * jnp.repeat(heights, dims[axis_at] // blocks).reshape([-1 if axis == axis_at else 1 for axis in range(len(dims))])
    return factor_of


def centred(stream_key, shape, width, reach, shards=(), kind=jnp.bfloat16):
    result = jax.random.normal(stream_key, shape, jnp.float32) * width
    if len(shards) > 0:
        result = levels(stream_key, shape, shards, -0.22, 0.18) * result
    return jnp.clip(result, min=-reach, max=reach).astype(kind)


def bell_draw_with(stream_key, extent, deviation, bound, split, heavy, kind=jnp.bfloat16):
    entries = deviation * jax.random.normal(stream_key, extent, jnp.float32)
    if split:
        entries = entries * levels(stream_key, extent, split, -0.22, 0.18)
    return jnp.clip(with_spikes(entries, jax.random.fold_in(stream_key, 3), *heavy), -bound, bound).astype(kind)


def setup_inputs(seed: int = 0) -> dict:
    seeds = jax.random.split(jax.random.key(seed), 6)
    return {
        "acts": centred(seeds[0], (2 * LAYERS, TOK, D // 2), 1.0, 6.0, ((0, 4), (2, 8))),
        "w_enc": centred(seeds[1], (2 * LAYERS, D // 2, LATENTS), (LAYERS * D) ** -0.5, 0.0625, ((0, 4), (2, 8))),
        "b_enc": centred(seeds[2], (LATENTS,), 0.5, 3.0, ((0, 8),), jnp.float32),
        "w_dec": bell_draw_with(seeds[3], (2 * LAYERS, LATENTS, D // 2), LATENTS ** -0.5, 0.125, ((0, 4), (1, 8)), (1, 2, 8, 2.0)),
        "b_dec": centred(seeds[4], (2 * LAYERS, D // 2), 0.5, 3.0, ((0, 4), (1, 8))),
    }


def reference(acts, w_enc, b_enc, w_dec, b_dec):
    half = D // 2
    full_acts = [jnp.concatenate([acts[2 * i], acts[2 * i + 1]], axis=1) for i in range(LAYERS)]
    full_enc = [jnp.concatenate([w_enc[2 * i], w_enc[2 * i + 1]], axis=0) for i in range(LAYERS)]
    full_dec = [jnp.concatenate([w_dec[2 * i], w_dec[2 * i + 1]], axis=1) for i in range(LAYERS)]
    full_bias = [jnp.concatenate([b_dec[2 * i], b_dec[2 * i + 1]], axis=0) for i in range(LAYERS)]
    pre = jnp.zeros((TOK, LATENTS), jnp.float32) + b_enc[None, :].astype(jnp.float32)
    for layer_idx in range(LAYERS):
        pre = pre + jnp.dot(full_acts[layer_idx], full_enc[layer_idx], preferred_element_type=jnp.float32)
    feat = (jax.nn.softplus(4.0 * pre) / 4.0).astype(jnp.bfloat16)
    scale = TOK ** -0.5
    grad_feat = jnp.zeros((TOK, LATENTS), jnp.float32)
    dec_list = []
    bdec_list = []
    for layer_idx in range(LAYERS):
        recon = jnp.dot(feat, full_dec[layer_idx], preferred_element_type=jnp.float32)
        err = (recon + full_bias[layer_idx][None, :].astype(jnp.float32) - full_acts[layer_idx].astype(jnp.float32)).astype(jnp.bfloat16)
        bias_grad = scale * jnp.sum(err.astype(jnp.float32), axis=0)
        bdec_list.append(bias_grad[:half])
        bdec_list.append(bias_grad[half:])
        dec_grad = (scale * jnp.dot(feat.T, err, preferred_element_type=jnp.float32)).astype(jnp.bfloat16)
        dec_list.append(dec_grad[:, :half])
        dec_list.append(dec_grad[:, half:])
        grad_feat = grad_feat + jnp.dot(err, full_dec[layer_idx].T, preferred_element_type=jnp.float32)
    grad_feat = scale * grad_feat
    grad_pre = grad_feat * jax.nn.sigmoid(4.0 * pre)
    grad_benc = jnp.sum(grad_pre, axis=0)
    grad_pre_b = grad_pre.astype(jnp.bfloat16)
    enc_list = []
    for layer_idx in range(LAYERS):
        enc_grad = jnp.dot(full_acts[layer_idx].T, grad_pre_b, preferred_element_type=jnp.float32).astype(jnp.bfloat16)
        enc_list.append(enc_grad[:half])
        enc_list.append(enc_grad[half:])
    return jnp.stack(enc_list), jnp.stack(dec_list), grad_benc, jnp.stack(bdec_list)
```

```python
import functools

import jax
import jax.numpy as jnp
from jax import lax
from jax.experimental import pallas as pl
from jax.experimental.pallas import tpu as pltpu
from jax.sharding import PartitionSpec as P

MESH = pl.DeviceIdType.MESH
F32 = jnp.float32
BF16 = jnp.bfloat16
INNER = 2


def place(n):
    me = lax.axis_index("latent")
    return me // INNER, lax.rem(me, INNER), n // INNER


def greet(n):
    z, y, depth = place(n)
    barrier = pltpu.get_barrier_semaphore()

    def signal(index):
        pl.semaphore_signal(barrier, inc=1, device_id={"latent": index}, device_id_type=MESH)

    signal(z * INNER + 1 - y)

    @pl.when(z > 0)
    def _():
        signal((z - 1) * INNER + y)

    @pl.when(z < depth - 1)
    def _():
        signal((z + 1) * INNER + y)

    peers = 1 + jnp.where(z > 0, 1, 0) + jnp.where(z < depth - 1, 1, 0)
    pl.semaphore_wait(barrier, peers)


def remote(src, dst, send, recv, index, axis="latent"):
    return pltpu.make_async_remote_copy(
        src_ref=src,
        dst_ref=dst,
        send_sem=send,
        recv_sem=recv,
        device_id={axis: index},
        device_id_type=MESH,
    )


def gather_kernel(n, view_in, view, x_ref, out_ref, local_sem, send, recv):
    z, y, depth = place(n)
    greet(n)
    me = z * INNER + y
    partner = z * INNER + 1 - y

    def move(h, block, way, own, start):
        src = view_in(x_ref, h) if own else view(out_ref, block, h)
        target = (partner, me + INNER, me - INNER)[way]
        copy = remote(src, view(out_ref, block, h), send.at[way, h, block], recv.at[h, block], target)
        if start:
            copy.start()
        else:
            copy.wait_send()

    def along(h, block, own, start, up=True, down=True):
        if up:

            @pl.when(z < depth - 1)
            def _():
                move(h, block, 1, own, start)

        if down:

            @pl.when(z > 0)
            def _():
                move(h, block, 2, own, start)

    def arrive(h, block):
        spot = view(out_ref, block, h)
        remote(spot, spot, send.at[0, h, block], recv.at[h, block], partner).wait_recv()

    def run(start):
        move(1, me, 0, True, start)
        along(0, me, True, start)
        along(1, me, True, start)
        move(0, me, 0, True, start)
        if start:
            keep = [
                pltpu.make_async_copy(view_in(x_ref, h), view(out_ref, me, h), local_sem.at[h])
                for h in range(2)
            ]
            for copy in keep:
                copy.start()
            arrive(1, partner)
        along(1, partner, False, start)
        for d in range(1, depth):
            for below in (True, False):
                at = z - d if below else z + d

                @pl.when(at >= 0 if below else at < depth)
                def _():
                    for h, side in ((0, y), (1, y), (1, 1 - y)):
                        block = at * INNER + side
                        if start:
                            arrive(h, block)
                        along(h, block, False, start, up=below, down=not below)
                        if h == 0:
                            move(0, block, 0, False, start)

        if start:
            for copy in keep:
                copy.wait()
            for at in range(depth):
                arrive(0, at * INNER + 1 - y)

    run(True)
    run(False)


def gather_blocks(x, n, by_rows, collective_id):
    rows, width = x.shape
    if by_rows:
        shape, half = (n * rows, width), width // 2
        flat = rows % 16 == 0 and half % 128 == 0
        blocks = (rows, half)
        view_in = lambda ref, h: ref.at[:, pl.ds(h * half, half)]
        view = lambda ref, j, h: ref.at[
            pl.ds(pl.multiple_of(j * rows, rows), rows), pl.ds(h * half, half)
        ]
    else:
        shape, half = (rows, n * width), rows // 2
        flat = width % 128 == 0 and half % 16 == 0
        blocks = (half, width)
        view_in = lambda ref, h: ref.at[pl.ds(h * half, half), :]
        view = lambda ref, j, h: ref.at[
            pl.ds(h * half, half), pl.ds(pl.multiple_of(j * width, width), width)
        ]
    if not flat:
        if by_rows:
            x = x.reshape(rows, 2, half).transpose(1, 0, 2)
        else:
            x = x.reshape(2, half, width)
        shape = (n, 2) + blocks
        view_in = lambda ref, h: ref.at[h]
        view = lambda ref, j, h: ref.at[j, h]
    out = pl.pallas_call(
        functools.partial(gather_kernel, n, view_in, view),
        out_shape=jax.ShapeDtypeStruct(shape, x.dtype),
        in_specs=[pl.BlockSpec(memory_space=pltpu.VMEM)],
        out_specs=pl.BlockSpec(memory_space=pltpu.VMEM),
        scratch_shapes=[
            pltpu.SemaphoreType.DMA((2,)),
            pltpu.SemaphoreType.DMA((3, 2, n)),
            pltpu.SemaphoreType.DMA((2, n)),
        ],
        compiler_params=pltpu.CompilerParams(collective_id=collective_id, has_side_effects=True),
        name="gather_rows" if by_rows else "gather_columns",
    )(x)
    if flat:
        return out
    if by_rows:
        return out.transpose(0, 2, 1, 3).reshape(n * rows, width)
    return out.transpose(1, 2, 0, 3).reshape(rows, n * width)


def scatter_kernel(
    n, view, part, out_ref, side_in, up_in, down_in, up_out, down_out, last_in, last_out,
    side_sem, up_sem, down_sem, last_sem,
):
    z, y, depth = place(n)
    greet(n)
    me = z * INNER + y
    partner = z * INNER + 1 - y

    def side_copy(at):
        return remote(
            view(part, at * INNER + 1 - y, 0), side_in.at[at],
            side_sem.at[0, at], side_sem.at[1, at], partner,
        )

    def line_copy(up, lane, at):
        stay, land, sems = (up_out, up_in, up_sem) if up else (down_out, down_in, down_sem)
        return remote(
            stay.at[lane, at], land.at[lane, at], sems.at[0, lane, at], sems.at[1, lane, at],
            me + INNER if up else me - INNER,
        )

    last_copy = remote(last_out, last_in, last_sem.at[0], last_sem.at[1], partner)

    for at in range(depth):
        side_copy(at).start()

    def own_term(lane, at):
        if lane < 2:
            return view(part, at * INNER + lane, 1)[...].astype(F32)
        return view(part, at * INNER + y, 0)[...].astype(F32) + side_in[at].astype(F32)

    for d in range(depth - 1, 0, -1):
        for lane in range(3):
            if lane == 2:
                for up in (True, False):
                    at = z + d if up else z - d

                    @pl.when(at < depth if up else at >= 0)
                    def _():
                        side_copy(at).wait_recv()

            for up in (True, False):
                at = z + d if up else z - d
                valid = at < depth if up else at >= 0
                inner = z > 0 if up else z < depth - 1
                stay, land = (up_out, up_in) if up else (down_out, down_in)

                @pl.when(jnp.logical_and(valid, inner))
                def _():
                    line_copy(up, lane, at).wait_recv()
                    stay[lane, at] = (own_term(lane, at) + land[lane, at].astype(F32)).astype(BF16)

                @pl.when(jnp.logical_and(valid, jnp.logical_not(inner)))
                def _():
                    stay[lane, at] = own_term(lane, at).astype(BF16)

                @pl.when(valid)
                def _():
                    line_copy(up, lane, at).start()

    side_copy(z).wait_recv()

    @pl.when(z > 0)
    def _():
        for lane in range(3):
            line_copy(True, lane, z).wait_recv()

    @pl.when(z == 0)
    def _():
        for lane in range(3):
            up_in[lane, z] = jnp.zeros(up_in.shape[2:], BF16)

    @pl.when(z < depth - 1)
    def _():
        for lane in range(3):
            line_copy(False, lane, z).wait_recv()

    @pl.when(z == depth - 1)
    def _():
        for lane in range(3):
            down_in[lane, z] = jnp.zeros(down_in.shape[2:], BF16)

    def both(lane):
        return up_in[lane, z].astype(F32) + down_in[lane, z].astype(F32)

    other = 1 - y
    last_out[...] = (view(part, partner, 1)[...].astype(F32) + both(other)).astype(BF16)
    last_copy.start()
    out_ref[0] = own_term(2, z) + both(2)
    last_copy.wait_recv()
    out_ref[1] = view(part, me, 1)[...].astype(F32) + both(y) + last_in[...].astype(F32)
    last_copy.wait_send()
    for at in range(depth):
        side_copy(at).wait_send()
    for d in range(depth - 1, 0, -1):
        for up in (True, False):
            at = z + d if up else z - d

            @pl.when(at < depth if up else at >= 0)
            def _():
                for lane in range(3):
                    line_copy(up, lane, at).wait_send()


def scatter_sum(x, n, collective_id):
    tokens, width = x.shape
    rows, half, depth = tokens // n, width // 2, n // INNER
    flat = rows % 16 == 0 and half % 128 == 0
    if flat:
        view = lambda ref, j, h: ref.at[
            pl.ds(pl.multiple_of(j * rows, rows), rows), pl.ds(h * half, half)
        ]
    else:
        x = x.reshape(n, rows, 2, half).transpose(0, 2, 1, 3)
        view = lambda ref, j, h: ref.at[j, h]
    line = pltpu.VMEM((3, depth, rows, half), BF16)
    out = pl.pallas_call(
        functools.partial(scatter_kernel, n, view),
        out_shape=jax.ShapeDtypeStruct((2, rows, half), F32),
        in_specs=[pl.BlockSpec(memory_space=pltpu.VMEM)],
        out_specs=pl.BlockSpec(memory_space=pltpu.VMEM),
        scratch_shapes=[
            pltpu.VMEM((depth, rows, half), BF16),
            line, line, line, line,
            pltpu.VMEM((rows, half), BF16),
            pltpu.VMEM((rows, half), BF16),
            pltpu.SemaphoreType.DMA((2, depth)),
            pltpu.SemaphoreType.DMA((2, 3, depth)),
            pltpu.SemaphoreType.DMA((2, 3, depth)),
            pltpu.SemaphoreType.DMA((2,)),
        ],
        compiler_params=pltpu.CompilerParams(collective_id=collective_id, has_side_effects=True),
        name="scatter_sum",
    )(x)
    return jnp.concatenate([out[0], out[1]], axis=1)


def reduce_kernel(part, out_ref, pair_in, far_in, far_out, sems):
    place_own = lax.axis_index("layer")
    core = lax.rem(place_own, 2)
    pair = place_own + 1 - 2 * core
    far = lax.rem(place_own + 2, 4)
    barrier = pltpu.get_barrier_semaphore()
    for index in (pair, far):
        pl.semaphore_signal(barrier, inc=1, device_id={"layer": index}, device_id_type=MESH)
    pl.semaphore_wait(barrier, 2)
    first = remote(part.at[1 - core], pair_in, sems.at[0], sems.at[1], pair, "layer")
    first.start()
    first.wait_recv()
    far_out[...] = (part[core].astype(F32) + pair_in[...].astype(F32)).astype(BF16)
    second = remote(far_out, far_in, sems.at[2], sems.at[3], far, "layer")
    second.start()
    second.wait_recv()
    out_ref[core] = (far_out[...].astype(F32) + far_in[...].astype(F32)).astype(BF16)
    third = remote(out_ref.at[core], out_ref.at[core], sems.at[4], sems.at[5], pair, "layer")
    third.start()
    third.wait_recv()
    first.wait_send()
    second.wait_send()
    third.wait_send()


def layer_sum(x, collective_id):
    tokens, width = x.shape
    half = tokens // 2
    out = pl.pallas_call(
        reduce_kernel,
        out_shape=jax.ShapeDtypeStruct((2, half, width), BF16),
        in_specs=[pl.BlockSpec(memory_space=pltpu.VMEM)],
        out_specs=pl.BlockSpec(memory_space=pltpu.VMEM),
        scratch_shapes=[pltpu.VMEM((half, width), BF16)] * 3 + [pltpu.SemaphoreType.DMA((6,))],
        compiler_params=pltpu.CompilerParams(collective_id=collective_id, has_side_effects=True),
        name="layer_sum",
    )(x.reshape(2, half, width))
    return out.reshape(tokens, width).astype(F32)


def body(n, acts, w_enc, b_enc, w_dec, b_dec):
    local = acts[0]
    width_own = local.shape[1]
    enc_own = w_enc[0]
    dec_own = w_dec[0]
    full = gather_blocks(local, n, False, 0)
    tokens_all = full.shape[0]
    scale = tokens_all ** (-0.5)
    position = lax.axis_index("latent")
    rows = tokens_all // n
    part = jnp.dot(full, enc_own, preferred_element_type=F32).astype(BF16)
    pre = layer_sum(part, 1) + b_enc[None, :]
    feat = (jax.nn.softplus(4.0 * pre) / 4.0).astype(BF16)
    bias_own = lax.dynamic_update_slice(
        jnp.zeros((1, n * width_own), F32), b_dec.astype(F32), (0, position * width_own)
    )
    term = jnp.dot(feat, dec_own, preferred_element_type=F32) + bias_own
    recon = scatter_sum(term.astype(BF16), n, 2)
    own_rows = lax.dynamic_slice_in_dim(full, position * rows, rows, 0)
    err_rows = (recon - own_rows.astype(F32)).astype(BF16)
    err = gather_blocks(err_rows, n, True, 3)
    bias_grad_full = scale * jnp.sum(err.astype(F32), axis=0)
    grad_bdec = lax.dynamic_slice_in_dim(bias_grad_full, position * width_own, width_own, 0)
    dec_prod = lax.dot_general(
        feat, err, (((0,), (0,)), ((), ())), preferred_element_type=F32
    )
    grad_dec = (scale * dec_prod).astype(BF16)
    feat_term = lax.dot_general(
        err, dec_own, (((1,), (1,)), ((), ())), preferred_element_type=F32
    )
    grad_feat = scale * layer_sum(feat_term.astype(BF16), 4)
    grad_pre = grad_feat * jax.nn.sigmoid(4.0 * pre)
    grad_benc = jnp.sum(grad_pre, axis=0)
    grad_pre_b = grad_pre.astype(BF16)
    enc_prod = lax.dot_general(
        full, grad_pre_b, (((0,), (0,)), ((), ())), preferred_element_type=F32
    )
    grad_enc = enc_prod.astype(BF16)
    return (grad_enc[None], grad_dec[None], grad_benc, grad_bdec[None])


def solution(mesh):
    return jax.shard_map(
        functools.partial(body, mesh.shape["latent"]),
        mesh=mesh,
        in_specs=(
            P("layer", None, "latent"),
            P("layer", None, "latent"),
            P("latent"),
            P("layer", "latent", None),
            P("layer", "latent"),
        ),
        out_specs=(
            P("layer", None, "latent"),
            P("layer", "latent", None),
            P("latent"),
            P("layer", "latent"),
        ),
        check_vma=False,
    )
```
